32 devices in a mesh: outer: 4 (over y, core), inner: 8 (over z, x).
Axes of the slice: x: 2, y: 2, z: 4, core: 2. Of those that a mesh axis runs over, the one named last changes fastest.
Arguments:
- queries: bfloat16 [4096, 2048], P(('outer', 'inner')), may hold values from -2 to 2
- keys: bfloat16 [4096, 2048], P(('outer', 'inner')), may hold values from -2 to 2
- values: bfloat16 [4096, 2048], P(('outer', 'inner')), may hold values from -6 to 6
- grad_out: bfloat16 [4096, 2048], P(('outer', 'inner')), may hold values from -96 to 96
- window: int32 [1], replicated, may hold values from 513 to 640
Outputs:
- query_grad: bfloat16 [4096, 2048], P(('outer', 'inner'))
- key_grad: bfloat16 [4096, 2048], P(('outer', 'inner'))
- value_grad: bfloat16 [4096, 2048], P(('outer', 'inner'))
The draws below stay inside these ranges and needn't reach their ends.
All inputs are finite; a program needn't handle non-finite values.
Results may differ from the reference program's by a relative error of at most 0.0085.
Values may be sent and summed in bfloat16 or wider, within the bound.
A program may use at most 64 MiB of HBM per device.

```python
import jax
import jax.numpy as jnp
from jax import lax

TOK_DEV = 128
HEADS = 16
HD = 128
TOKENS = 4096


def shard_levels(own_key, shape, cuts, smallest, largest):
    loudness = 1.0
    for axis_at, blocks in cuts:
        heights = jax.random.uniform(jax.random.fold_in(jax.random.fold_in(own_key, 6), axis_at), (blocks,), jnp.float32, smallest / len(cuts), largest / len(cuts))
        loudness = loudness * jnp.repeat(jnp.exp(heights), shape[axis_at] // blocks).reshape((-1,) + (1,) * (len(shape) - 1 - axis_at))
    return loudness


def centred(stream_key, dims, scale, bound, cuts=(), kind=jnp.bfloat16):
    factor_of = shard_levels(stream_key, dims, cuts, -0.22, 0.18) if cuts else 1.0
    array = jax.random.normal(stream_key, dims, jnp.float32) * scale * factor_of
    return jnp.minimum(jnp.maximum(array, -bound), bound).astype(kind)


def setup_inputs(seed: int = 0) -> dict:
    splits = jax.random.split(jax.random.key(seed), 6)
    return {
        "queries": jnp.clip(jax.random.uniform(splits[0], (TOKENS, HEADS * HD), jnp.float32, -2.0, 2.0) * shard_levels(splits[0], (TOKENS, HEADS * HD), ((0, 32),), -0.4, 0.0), -2.0, 2.0).astype(jnp.bfloat16),
        "keys": jnp.clip(jax.random.uniform(splits[1], (TOKENS, HEADS * HD), jnp.float32, -2.0, 2.0) * shard_levels(splits[1], (TOKENS, HEADS * HD), ((0, 32),), -0.4, 0.0), -2.0, 2.0).astype(jnp.bfloat16),
        "values": centred(splits[2], (TOKENS, HEADS * HD), 1.0, 6.0, ((0, 32),)),
        "grad_out": centred(splits[3], (TOKENS, HEADS * HD), 16.0, 96.0, ((0, 32),)),
        "window": jax.random.randint(splits[4], (1,), 4 * TOK_DEV + 1, 5 * TOK_DEV + 1).astype(jnp.int32),
    }


def reference(queries, keys, values, grad_out, window):
    count = TOK_DEV
    shards = TOKENS // count
    scale = HD ** -0.5
    width = window[0]
    query_all = queries.reshape(TOKENS, HEADS, HD)
    grad_all = grad_out.reshape(TOKENS, HEADS, HD)
    filler = jnp.zeros((5 * count, HEADS * HD), keys.dtype)
    key_pad = jnp.concatenate([filler, keys], axis=0).reshape(-1, HEADS, HD)
    value_pad = jnp.concatenate([filler, values], axis=0).reshape(-1, HEADS, HD)

    def step(carry, index):
        key_acc, value_acc = carry
        begin = (index * count).astype(jnp.int32)
        query_block = lax.dynamic_slice_in_dim(query_all, begin, count, 0).astype(jnp.float32)
        grad_block = lax.dynamic_slice_in_dim(grad_all, begin, count, 0).astype(jnp.float32)
        key_block = lax.dynamic_slice_in_dim(key_pad, begin, 6 * count, 0).astype(jnp.float32)
        value_block = lax.dynamic_slice_in_dim(value_pad, begin, 6 * count, 0).astype(jnp.float32)
        query_pos = begin + jnp.arange(count, dtype=jnp.int32)[:, None]
        key_pos = begin - 5 * count + jnp.arange(6 * count, dtype=jnp.int32)[None, :]
        allowed = (key_pos <= query_pos) & (key_pos > query_pos - width) & (key_pos >= 0)
        logits = jnp.einsum("qhd,khd->hqk", query_block, key_block) * scale
        weights = jnp.where(allowed[None], jnp.exp(logits), jnp.float32(0.0))
        norm_total = jnp.sum(weights, axis=2)
        weights_low = lax.optimization_barrier(weights.astype(jnp.bfloat16)).astype(jnp.float32)
        weighted = jnp.einsum("hqk,khd->qhd", weights_low, value_block)
        output = weighted / jnp.transpose(norm_total)[:, :, None]
        centre = jnp.transpose(jnp.sum(grad_block * output, axis=2))
        log_norm = jnp.log(norm_total)
        probs = jnp.where(allowed[None], jnp.exp(logits - log_norm[:, :, None]), jnp.float32(0.0))
        probs_low = lax.optimization_barrier(probs.astype(jnp.bfloat16)).astype(jnp.float32)
        prob_grad = jnp.einsum("qhd,khd->hqk", grad_block, value_block)
        logit_grad = probs * (prob_grad - centre[:, :, None])
        logit_low = lax.optimization_barrier(logit_grad.astype(jnp.bfloat16)).astype(jnp.float32)
        logit_split = logit_low.reshape(HEADS, count, 6, count)
        probs_split = probs_low.reshape(HEADS, count, 6, count)
        key_split = key_block.reshape(6, count, HEADS, HD)
        query_terms = (jnp.einsum("hqec,echd->eqhd", logit_split, key_split) * scale).astype(jnp.bfloat16)
        query_sum = jnp.sum(query_terms.astype(jnp.float32), axis=0)
        key_terms = (jnp.einsum("hqec,qhd->echd", logit_split, query_block) * scale).astype(jnp.bfloat16)
        value_terms = jnp.einsum("hqec,qhd->echd", probs_split, grad_block).astype(jnp.bfloat16)
        key_terms = key_terms.astype(jnp.float32).reshape(6 * count, HEADS, HD)
        value_terms = value_terms.astype(jnp.float32).reshape(6 * count, HEADS, HD)
        key_acc = lax.dynamic_update_slice_in_dim(key_acc, lax.dynamic_slice_in_dim(key_acc, begin, 6 * count, 0) + key_terms, begin, 0)
        value_acc = lax.dynamic_update_slice_in_dim(value_acc, lax.dynamic_slice_in_dim(value_acc, begin, 6 * count, 0) + value_terms, begin, 0)
        return (key_acc, value_acc), query_sum.astype(jnp.bfloat16)

    start_acc = jnp.zeros(((shards + 5) * count, HEADS, HD), jnp.float32)
    carry, query_parts = lax.scan(step, (start_acc, start_acc), jnp.arange(shards, dtype=jnp.int32))
    key_acc, value_acc = carry
    query_grad = query_parts.reshape(TOKENS, HEADS * HD)
    key_grad = key_acc[5 * count:].reshape(TOKENS, HEADS * HD).astype(jnp.bfloat16)
    value_grad = value_acc[5 * count:].reshape(TOKENS, HEADS * HD).astype(jnp.bfloat16)
    return (query_grad, key_grad, value_grad)
```

```python
import functools

import jax
import jax.numpy as jnp
from jax import lax
from jax.experimental import pallas as pl
from jax.experimental.pallas import tpu as pltpu
from jax.sharding import PartitionSpec as P

HD = 128
LINE = 4
GROUP = 1
MESH = pl.DeviceIdType.MESH
NT = (((1,), (1,)), ((), ()))
NN = (((1,), (0,)), ((), ()))
TN = (((0,), (0,)), ((), ()))


def dot(a, b, dims):
    return lax.dot_general(a, b, dims, preferred_element_type=jnp.float32)


def kernel(
    sizes, window, q_ref, k_ref, v_ref, g_ref, dq_ref, dk_ref, dv_ref,
    qd, kv, slot, rout, acc, fin, w_s, p_s,
    xsend, xrecv, xloc, fsend, frecv, rsend, rrecv, osend, orecv, oloc,
):
    outer, inner, tok, heads = sizes
    half = heads // 2
    chunks = half // GROUP
    wide = GROUP * HD
    scale = HD ** -0.5
    total = outer * inner
    lines = total // (2 * LINE)
    me = lax.axis_index("outer") * inner + lax.axis_index("inner")
    x = lax.rem(me, 2)
    pair = me // 2
    z = lax.rem(pair, LINE)
    line = pair // LINE

    def dev(to_line, to_z, to_x):
        s = (to_line * LINE + to_z) * 2 + to_x
        return (s // inner, lax.rem(s, inner))

    partner = dev(line, z, 1 - x)
    up = dev(line, lax.rem(z + 1, LINE), x)
    down = dev(line, lax.rem(z + LINE - 1, LINE), x)
    ahead = dev(lax.rem(line + 1, lines), lax.rem(z + LINE - 1, LINE), x)
    behind = dev(lax.rem(line + lines - 1, lines), lax.rem(z + 1, LINE), x)
    low = z >= 1
    high = z <= LINE - 2

    ins = (k_ref, v_ref, q_ref, g_ref)
    outs = (dq_ref, dk_ref, dv_ref)

    def cols(side, c):
        return pl.ds(pl.multiple_of((side * half + c * GROUP) * HD, HD), wide)

    my_rows = pl.ds(pl.multiple_of(x * tok, tok), tok)
    other_rows = pl.ds(pl.multiple_of((1 - x) * tok, tok), tok)

    def landing(i, c):
        return kv.at[0, c, i, my_rows, :] if i < 2 else qd.at[c, i - 2, my_rows, :]

    def local_in(i, c):
        return pltpu.make_async_copy(ins[i].at[:, cols(x, c)], landing(i, c), xloc.at[c, i])

    def cross_in(i, c):
        return pltpu.make_async_remote_copy(
            ins[i].at[:, cols(1 - x, c)], landing(i, c), xsend.at[c, i], xrecv.at[c, i],
            device_id=partner, device_id_type=MESH)

    def local_out(i, c):
        return pltpu.make_async_copy(
            fin.at[c, i, my_rows, :], outs[i].at[:, cols(x, c)], oloc.at[c, i])

    def cross_out(i, c):
        return pltpu.make_async_remote_copy(
            fin.at[c, i, other_rows, :], outs[i].at[:, cols(x, c)], osend.at[c, i],
            orecv.at[c, i], device_id=partner, device_id_type=MESH)

    def forward(c, src, dst, sem, to):
        return pltpu.make_async_remote_copy(
            kv.at[src, c], kv.at[dst, c], fsend.at[c, sem], frecv.at[c, dst - 1],
            device_id=to, device_id_type=MESH)

    def back(c, d, dst, to):
        return pltpu.make_async_remote_copy(
            rout.at[d - 1, c], slot.at[dst, c], rsend.at[c, d - 1], rrecv.at[c, dst],
            device_id=to, device_id_type=MESH)

    def arrived(c, d):
        forward(c, 0, d, 0, up).wait_recv()

    def returned(c, dst):
        back(c, 1, dst, up).wait_recv()

    def every_chunk(body):
        def step(c, carry):
            body(c)
            return carry
        lax.fori_loop(0, chunks, step, 0)

    @every_chunk
    def _(c):
        for i in range(4):
            local_in(i, c).start()

    barrier = pltpu.get_barrier_semaphore()
    pl.semaphore_signal(barrier, inc=1, device_id=partner, device_id_type=MESH)
    for cond, targets in ((high, (up, behind)), (low, (down, ahead))):
        @pl.when(cond)
        def _():
            for target in targets:
                pl.semaphore_signal(barrier, inc=1, device_id=target, device_id_type=MESH)
    pl.semaphore_wait(barrier, 1 + 2 * high.astype(jnp.int32) + 2 * low.astype(jnp.int32))

    @every_chunk
    def _(c):
        for i in range(4):
            cross_in(i, c).start()

    def when(*conds):
        return pl.when(functools.reduce(jnp.logical_and, conds))

    def stage_a(c):
        for i in range(2):
            local_in(i, c).wait()
            cross_in(i, c).wait_recv()

        @when(high)
        def _():
            forward(c, 0, 1, 0, up).start()

        @when(low)
        def _():
            forward(c, 0, 3, 1, ahead).start()

    def stage_b1(c):
        @when(low)
        def _():
            arrived(c, 1)

            @when(high)
            def _():
                forward(c, 1, 2, 2, up).start()

        @when(high)
        def _():
            arrived(c, 3)

            @when(low)
            def _():
                forward(c, 3, 2, 3, down).start()

    def stage_b2(c):
        arrived(c, 2)

        @when(z == 2)
        def _():
            forward(c, 2, 3, 4, up).start()

        @when(z == 1)
        def _():
            forward(c, 2, 1, 4, down).start()

    def stage_c(c):
        for i in range(2, 4):
            local_in(i, c).wait()
            cross_in(i, c).wait_recv()

        @when(z == LINE - 1)
        def _():
            arrived(c, 3)

        @when(z == 0)
        def _():
            arrived(c, 1)

        width = window[0]
        size = 2 * tok
        for h in range(GROUP):
            hs = slice(h * HD, (h + 1) * HD)
            query, grad = qd[c, 0, :, hs], qd[c, 1, :, hs]
            norm = jnp.zeros((1, size), jnp.float32)
            mixed = jnp.zeros((1, size), jnp.float32)
            for d in range(4):
                rows, top = (size, 0) if d < 3 else (tok, tok)
                key, value = kv[d, c, 0, top:, hs], kv[d, c, 1, top:, hs]
                logits = dot(key, query[:rows], NT) * scale
                shape = (rows, rows)
                delta = (
                    lax.broadcasted_iota(jnp.int32, shape, 1)
                    - lax.broadcasted_iota(jnp.int32, shape, 0)
                    + (d * size - top)
                )
                reach = jnp.where(pair >= d, width, 0)
                allowed = (delta >= 0) & (delta < reach) if d == 0 else delta < reach
                weights = jnp.where(allowed, jnp.exp(logits), 0.0)
                prob_grad = dot(value, grad[:rows], NT)
                w_s[d, :rows, :rows] = weights
                p_s[d, :rows, :rows] = prob_grad
                norm_part = jnp.sum(weights, axis=0, keepdims=True)
                mixed_part = jnp.sum(weights * prob_grad, axis=0, keepdims=True)
                if d == 3:
                    rest = jnp.zeros((1, size - tok), jnp.float32)
                    norm_part = jnp.concatenate([norm_part, rest], axis=1)
                    mixed_part = jnp.concatenate([mixed_part, rest], axis=1)
                norm = norm + norm_part
                mixed = mixed + mixed_part
            inverse = 1.0 / norm
            centre = mixed * inverse
            query_total = jnp.zeros((size, HD), jnp.float32)
            for d in range(4):
                rows, top = (size, 0) if d < 3 else (tok, tok)
                probs = w_s[d, :rows, :rows] * inverse[:, :rows]
                logit_grad = probs * (p_s[d, :rows, :rows] - centre[:, :rows])
                logit_grad = logit_grad.astype(jnp.bfloat16)
                acc[c, d, 1, top:, hs] = dot(probs.astype(jnp.bfloat16), grad[:rows], NN)
                acc[c, d, 0, top:, hs] = dot(logit_grad, query[:rows], NN) * scale
                part = dot(logit_grad, kv[d, c, 0, top:, hs], TN)
                if d == 3:
                    acc[c, d, :, :top, hs] = jnp.zeros((2, top, HD), jnp.float32)
                    part = jnp.concatenate([part, jnp.zeros((size - tok, HD), jnp.float32)], axis=0)
                query_total = query_total + part
            fin[c, 0, :, hs] = (query_total * scale).astype(jnp.bfloat16)
        local_out(0, c).start()
        cross_out(0, c).start()

        @when(z == LINE - 1)
        def _():
            rout[2, c] = acc[c, 3].astype(jnp.bfloat16)
            back(c, 3, 2, down).start()

        @when(z == 0)
        def _():
            rout[0, c] = acc[c, 1].astype(jnp.bfloat16)
            back(c, 1, 2, up).start()

    def fold(c, d, has_child, source):
        @when(has_child)
        def _():
            returned(c, source)
            rout[d - 1, c] = (acc[c, d] + slot[source, c].astype(jnp.float32)).astype(jnp.bfloat16)

        @when(jnp.logical_not(has_child))
        def _():
            rout[d - 1, c] = acc[c, d].astype(jnp.bfloat16)

    def stage_r2(c):
        fold(c, 2, jnp.logical_and(low, high), 2)

        @when(z >= 2)
        def _():
            back(c, 2, 1, down).start()

        @when(z < 2)
        def _():
            back(c, 2, 3, up).start()

    def stage_r1(c):
        @when(low)
        def _():
            fold(c, 1, high, 1)
            back(c, 1, 0, down).start()

        @when(high)
        def _():
            fold(c, 3, low, 3)
            back(c, 3, 4, behind).start()

    def stage_r0(c):
        @when(high)
        def _():
            returned(c, 0)
            acc[c, 0] = acc[c, 0] + slot[0, c].astype(jnp.float32)

        @when(low)
        def _():
            returned(c, 4)
            acc[c, 0] = acc[c, 0] + slot[4, c].astype(jnp.float32)

        fin[c, 1:] = acc[c, 0].astype(jnp.bfloat16)
        for i in range(1, 3):
            local_out(i, c).start()
            cross_out(i, c).start()

    stages = (stage_a, stage_b1, stage_b2, stage_c, stage_r2, stage_r1, stage_r0)

    def tick(t, carry):
        for lag, stage in enumerate(stages):
            c = t - lag

            @when(c >= 0, c < chunks)
            def _():
                stage(c)
        return carry

    lax.fori_loop(0, chunks + len(stages) - 1, tick, 0)

    @every_chunk
    def _(c):
        for i in range(4):
            cross_in(i, c).wait_send()
        for i in range(3):
            local_out(i, c).wait()
            cross_out(i, c).wait()

        @when(high)
        def _():
            forward(c, 0, 1, 0, up).wait_send()

        @when(low)
        def _():
            forward(c, 0, 3, 1, ahead).wait_send()

        @when(low, high)
        def _():
            forward(c, 1, 2, 2, up).wait_send()
            forward(c, 3, 2, 3, down).wait_send()
            forward(c, 2, 3, 4, up).wait_send()
        for d in range(1, 4):
            back(c, d, 0, up).wait_send()


def per_device(queries, keys, values, grad_out, window):
    outer, inner = lax.axis_size("outer"), lax.axis_size("inner")
    tok, columns = queries.shape
    heads = columns // HD
    half = heads // 2
    chunks = half // GROUP
    wide = GROUP * HD
    size = 2 * tok
    low, full = jnp.bfloat16, jnp.float32
    vmem = pl.BlockSpec(memory_space=pltpu.VMEM)
    block = (chunks, 2, size, wide)
    sems = (4, 4, 4, 5, 3, 3, 5, 3, 3, 3)
    return pl.pallas_call(
        functools.partial(kernel, (outer, inner, tok, heads)),
        out_shape=[jax.ShapeDtypeStruct((tok, columns), low)] * 3,
        in_specs=[pl.BlockSpec(memory_space=pltpu.SMEM)] + [vmem] * 4,
        out_specs=[vmem] * 3,
        scratch_shapes=[
            pltpu.VMEM(block, low),
            pltpu.VMEM((4,) + block, low),
            pltpu.VMEM((5,) + block, low),
            pltpu.VMEM((3,) + block, low),
            pltpu.VMEM((chunks, 4, 2, size, wide), full),
            pltpu.VMEM((chunks, 3, size, wide), low),
            pltpu.VMEM((4, size, size), full),
            pltpu.VMEM((4, size, size), full),
        ] + [pltpu.SemaphoreType.DMA((chunks, n)) for n in sems],
        compiler_params=pltpu.CompilerParams(
            collective_id=0, has_side_effects=True, vmem_limit_bytes=56 * 2**20
        ),
    )(window, queries, keys, values, grad_out)


def solution(mesh):
    rows = P(("outer", "inner"), None)
    return jax.shard_map(
        per_device,
        mesh=mesh,
        in_specs=(rows, rows, rows, rows, P()),
        out_specs=(rows, rows, rows),
        check_vma=False,
    )
```

```python
import functools

import jax
import jax.numpy as jnp
from jax import lax
from jax.experimental import pallas as pl
from jax.experimental.pallas import tpu as pltpu
from jax.sharding import PartitionSpec as P

HD = 128
LINE = 4
MESH = pl.DeviceIdType.MESH
NT = (((1,), (1,)), ((), ()))
NN = (((1,), (0,)), ((), ()))
TN = (((0,), (0,)), ((), ()))


def dot(a, b, dims):
    return lax.dot_general(a, b, dims, preferred_element_type=jnp.float32)


def kernel(
    sizes, window, q_ref, k_ref, v_ref, g_ref, dq_ref, dk_ref, dv_ref,
    qg, kv, slot, rout, acc, fin, w_s, p_s, part_out, part_in, whole_out, whole_in,
    xsend, xrecv, xloc, fsend, frecv, rsend, rrecv, osend, orecv, oloc, psend, precv, tsend, trecv,
):
    outer, inner, tok, heads = sizes
    half = heads // 2
    chunks = half
    size = 2 * tok
    scale = HD ** -0.5
    total = outer * inner
    pairs = total // 2
    me = lax.axis_index("outer") * inner + lax.axis_index("inner")
    x = lax.rem(me, 2)
    pair = me // 2
    z = LINE - 1 - lax.rem(pair, LINE)

    def dev(steps, to_x):
        s = lax.rem(pair + steps + pairs, pairs) * 2 + to_x
        return (s // inner, lax.rem(s, inner))

    partner = dev(0, 1 - x)
    up = dev(-1, x)
    down = dev(1, x)
    ahead = dev(-3, x)
    behind = dev(3, x)
    low = z >= 1
    high = z <= LINE - 2

    ins = (q_ref, g_ref, k_ref, v_ref)
    outs = (dq_ref, dk_ref, dv_ref)

    def cols(side, c):
        return pl.ds(pl.multiple_of((side * half + c) * HD, HD), HD)

    my_rows = pl.ds(pl.multiple_of(x * tok, tok), tok)
    other_rows = pl.ds(pl.multiple_of((1 - x) * tok, tok), tok)

    def landing(i, c):
        return qg.at[0, c, i, my_rows, :] if i < 2 else kv.at[c, i - 2, my_rows, :]

    def local_in(i, c):
        return pltpu.make_async_copy(ins[i].at[:, cols(x, c)], landing(i, c), xloc.at[c, i])

    def cross_in(i, c):
        return pltpu.make_async_remote_copy(
            ins[i].at[:, cols(1 - x, c)], landing(i, c), xsend.at[c, i], xrecv.at[c, i],
            device_id=partner, device_id_type=MESH)

    def local_out(i, c):
        return pltpu.make_async_copy(
            fin.at[c, i, my_rows, :], outs[i].at[:, cols(x, c)], oloc.at[c, i])

    def cross_out(i, c):
        return pltpu.make_async_remote_copy(
            fin.at[c, i, other_rows, :], outs[i].at[:, cols(x, c)], osend.at[c, i],
            orecv.at[c, i], device_id=partner, device_id_type=MESH)

    def forward(c, src, dst, sem, to):
        return pltpu.make_async_remote_copy(
            qg.at[src, c], qg.at[dst, c], fsend.at[c, sem], frecv.at[c, dst - 1],
            device_id=to, device_id_type=MESH)

    def back(c, d, dst, to):
        return pltpu.make_async_remote_copy(
            rout.at[d - 1, c], slot.at[dst, c], rsend.at[c, d - 1], rrecv.at[c, dst],
            device_id=to, device_id_type=MESH)

    def partial(c, d):
        return pltpu.make_async_remote_copy(
            part_out.at[c, d], part_in.at[c, d], psend.at[c, d - 1], precv.at[c, d - 1],
            device_id=dev(d, x), device_id_type=MESH)

    def totals(c, d):
        return pltpu.make_async_remote_copy(
            whole_out.at[c], whole_in.at[c, d], tsend.at[c, d - 1], trecv.at[c, d - 1],
            device_id=dev(-d, x), device_id_type=MESH)

    def arrived(c, d):
        forward(c, 0, d, 0, up).wait_recv()

    def returned(c, dst):
        back(c, 1, dst, up).wait_recv()

    def every_chunk(body):
        def step(c, carry):
            body(c)
            return carry
        lax.fori_loop(0, chunks, step, 0)

    @every_chunk
    def _(c):
        for i in range(4):
            local_in(i, c).start()

    barrier = pltpu.get_barrier_semaphore()
    for target in [partner] + [dev(d, x) for d in (-3, -2, -1, 1, 2, 3)]:
        pl.semaphore_signal(barrier, inc=1, device_id=target, device_id_type=MESH)
    pl.semaphore_wait(barrier, 7)

    @every_chunk
    def _(c):
        for i in range(4):
            cross_in(i, c).start()

    def when(*conds):
        return pl.when(functools.reduce(jnp.logical_and, conds))

    def stage_a(c):
        for i in range(2):
            local_in(i, c).wait()
            cross_in(i, c).wait_recv()

        @when(high)
        def _():
            forward(c, 0, 1, 0, up).start()

        @when(low)
        def _():
            forward(c, 0, 3, 1, ahead).start()

    def stage_b1(c):
        @when(low)
        def _():
            arrived(c, 1)

            @when(high)
            def _():
                forward(c, 1, 2, 2, up).start()

        @when(high)
        def _():
            arrived(c, 3)

            @when(low)
            def _():
                forward(c, 3, 2, 3, down).start()

    def stage_b2(c):
        arrived(c, 2)

        @when(z == 2)
        def _():
            forward(c, 2, 3, 4, up).start()

        @when(z == 1)
        def _():
            forward(c, 2, 1, 4, down).start()

    def stage_c(c):
        for i in range(2, 4):
            local_in(i, c).wait()
            cross_in(i, c).wait_recv()

        @when(z == LINE - 1)
        def _():
            arrived(c, 3)

        @when(z == 0)
        def _():
            arrived(c, 1)

        width = window[0]
        key_all, value_all = kv[c, 0], kv[c, 1]
        for d in range(4):
            rows, top = (size, 0) if d < 3 else (tok, tok)
            logits = dot(key_all[top:], qg[d, c, 0, :rows, :], NT) * scale
            shape = (rows, rows)
            delta = (
                lax.broadcasted_iota(jnp.int32, shape, 1)
                - lax.broadcasted_iota(jnp.int32, shape, 0)
                + (d * size - top)
            )
            reach = jnp.where(pair + d < pairs, width, 0)
            allowed = (delta >= 0) & (delta < reach) if d == 0 else delta < reach
            weights = jnp.where(allowed, jnp.exp(logits), 0.0)
            prob_grad = dot(value_all[top:], qg[d, c, 1, :rows, :], NT)
            w_s[c, d, :rows, :rows] = weights
            p_s[c, d, :rows, :rows] = prob_grad
            norm = jnp.sum(weights, axis=0, keepdims=True)
            mixed = jnp.sum(weights * prob_grad, axis=0, keepdims=True)
            if d == 3:
                part_out[c, d] = jnp.zeros((2, size), jnp.float32)
            part_out[c, d, 0:1, :rows] = norm
            part_out[c, d, 1:2, :rows] = mixed
            if d > 0:
                partial(c, d).start()

    def stage_s1(c):
        for d in range(1, 4):
            partial(c, d).wait_recv()
        sums = part_out[c, 0] + part_in[c, 1] + part_in[c, 2] + part_in[c, 3]
        inverse = 1.0 / sums[0:1]
        whole_out[c, 0:1] = inverse
        whole_out[c, 1:2] = sums[1:2] * inverse
        for d in range(1, 4):
            totals(c, d).start()

    def stage_s2(c):
        for d in range(1, 4):
            totals(c, d).wait_recv()
        key_all = kv[c, 0]
        key_total = jnp.zeros((size, HD), jnp.float32)
        value_total = jnp.zeros((size, HD), jnp.float32)
        for d in (3, 2, 1, 0):
            rows, top = (size, 0) if d < 3 else (tok, tok)
            stats = whole_in[c, d] if d else whole_out[c]
            probs = w_s[c, d, :rows, :rows] * stats[0:1, :rows]
            logit_grad = probs * (p_s[c, d, :rows, :rows] - stats[1:2, :rows])
            logit_grad = logit_grad.astype(jnp.bfloat16)
            value_part = dot(probs.astype(jnp.bfloat16), qg[d, c, 1, :rows, :], NN)
            key_part = dot(logit_grad, qg[d, c, 0, :rows, :], NN)
            if d == 3:
                acc[c, d, rows:, :] = jnp.zeros((size - rows, HD), jnp.float32)
                rest = jnp.zeros((top, HD), jnp.float32)
                value_part = jnp.concatenate([rest, value_part], axis=0)
                key_part = jnp.concatenate([rest, key_part], axis=0)
            value_total = value_total + value_part
            key_total = key_total + key_part
            acc[c, d, :rows, :] = dot(logit_grad, key_all[top:], TN) * scale
        fin[c, 1] = (key_total * scale).astype(jnp.bfloat16)
        fin[c, 2] = value_total.astype(jnp.bfloat16)

        @when(z == LINE - 1)
        def _():
            rout[2, c] = acc[c, 3].astype(jnp.bfloat16)
            back(c, 3, 2, down).start()

        @when(z == 0)
        def _():
            rout[0, c] = acc[c, 1].astype(jnp.bfloat16)
            back(c, 1, 2, up).start()

        for i in range(1, 3):
            local_out(i, c).start()
            cross_out(i, c).start()

    def fold(c, d, has_child, source):
        @when(has_child)
        def _():
            returned(c, source)
            rout[d - 1, c] = (acc[c, d] + slot[source, c].astype(jnp.float32)).astype(jnp.bfloat16)

        @when(jnp.logical_not(has_child))
        def _():
            rout[d - 1, c] = acc[c, d].astype(jnp.bfloat16)

    def stage_r2(c):
        fold(c, 2, jnp.logical_and(low, high), 2)

        @when(z >= 2)
        def _():
            back(c, 2, 1, down).start()

        @when(z < 2)
        def _():
            back(c, 2, 3, up).start()

    def stage_r1(c):
        @when(low)
        def _():
            fold(c, 1, high, 1)
            back(c, 1, 0, down).start()

        @when(high)
        def _():
            fold(c, 3, low, 3)
            back(c, 3, 4, behind).start()

    def stage_r0(c):
        @when(high)
        def _():
            returned(c, 0)
            acc[c, 0] = acc[c, 0] + slot[0, c].astype(jnp.float32)

        @when(low)
        def _():
            returned(c, 4)
            acc[c, 0] = acc[c, 0] + slot[4, c].astype(jnp.float32)

        fin[c, 0] = acc[c, 0].astype(jnp.bfloat16)
        local_out(0, c).start()
        cross_out(0, c).start()

    stages = (
        stage_a, stage_b1, stage_b2, stage_c, stage_s1, stage_s2, stage_r2, stage_r1, stage_r0
    )

    def tick(t, carry):
        for lag, stage in enumerate(stages):
            c = t - lag

            @when(c >= 0, c < chunks)
            def _():
                stage(c)
        return carry

    lax.fori_loop(0, chunks + len(stages) - 1, tick, 0)

    @every_chunk
    def _(c):
        for i in range(4):
            cross_in(i, c).wait_send()
        for i in range(3):
            local_out(i, c).wait()
            cross_out(i, c).wait()

        @when(high)
        def _():
            forward(c, 0, 1, 0, up).wait_send()

        @when(low)
        def _():
            forward(c, 0, 3, 1, ahead).wait_send()

        @when(low, high)
        def _():
            forward(c, 1, 2, 2, up).wait_send()
            forward(c, 3, 2, 3, down).wait_send()
            forward(c, 2, 3, 4, up).wait_send()
        for d in range(1, 4):
            back(c, d, 0, up).wait_send()
            partial(c, d).wait_send()
            totals(c, d).wait_send()


def per_device(queries, keys, values, grad_out, window):
    outer, inner = lax.axis_size("outer"), lax.axis_size("inner")
    tok, columns = queries.shape
    heads = columns // HD
    chunks = heads // 2
    size = 2 * tok
    low, full = jnp.bfloat16, jnp.float32
    vmem = pl.BlockSpec(memory_space=pltpu.VMEM)
    block = (chunks, 2, size, HD)
    sums = (chunks, size, HD)
    sems = (4, 4, 4, 5, 3, 3, 5, 3, 3, 3, 3, 3, 3, 3)
    return pl.pallas_call(
        functools.partial(kernel, (outer, inner, tok, heads)),
        out_shape=[jax.ShapeDtypeStruct((tok, columns), low)] * 3,
        in_specs=[pl.BlockSpec(memory_space=pltpu.SMEM)] + [vmem] * 4,
        out_specs=[vmem] * 3,
        scratch_shapes=[
            pltpu.VMEM((4,) + block, low),
            pltpu.VMEM(block, low),
            pltpu.VMEM((5,) + sums, low),
            pltpu.VMEM((3,) + sums, low),
            pltpu.VMEM((chunks, 4, size, HD), full),
            pltpu.VMEM((chunks, 3, size, HD), low),
            pltpu.VMEM((chunks, 4, size, size), full),
            pltpu.VMEM((chunks, 4, size, size), full),
            pltpu.VMEM((chunks, 4, 2, size), full),
            pltpu.VMEM((chunks, 4, 2, size), full),
            pltpu.VMEM((chunks, 2, size), full),
            pltpu.VMEM((chunks, 4, 2, size), full),
        ] + [pltpu.SemaphoreType.DMA((chunks, n)) for n in sems],
        compiler_params=pltpu.CompilerParams(
            collective_id=0, has_side_effects=True, vmem_limit_bytes=56 * 2**20
        ),
    )(window, queries, keys, values, grad_out)


def solution(mesh):
    rows = P(("outer", "inner"), None)
    return jax.shard_map(
        per_device,
        mesh=mesh,
        in_specs=(rows, rows, rows, rows, P()),
        out_specs=(rows, rows, rows),
        check_vma=False,
    )
```

```python
import functools

import jax
import jax.numpy as jnp
from jax import lax
from jax.experimental import pallas as pl
from jax.experimental.pallas import tpu as pltpu
from jax.sharding import PartitionSpec as P

HD = 128
LINE = 4
MESH = pl.DeviceIdType.MESH
NT = (((1,), (1,)), ((), ()))
NN = (((1,), (0,)), ((), ()))
TN = (((0,), (0,)), ((), ()))


def dot(a, b, dims):
    return lax.dot_general(a, b, dims, preferred_element_type=jnp.float32)


def kernel(
    sizes, window, q_ref, k_ref, v_ref, g_ref, dq_ref, dk_ref, dv_ref,
    qg, kv, slot, rout, acc, fin, w_s, p_s, part_out, part_in, whole_out, whole_in,
    xsend, xrecv, xloc, fsend, frecv, rsend, rrecv, osend, orecv, oloc, psend, precv, tsend, trecv,
):
    outer, inner, tok, heads = sizes
    half = heads // 2
    chunks = half
    size = 2 * tok
    scale = HD ** -0.5
    total = outer * inner
    pairs = total // 2
    me = lax.axis_index("outer") * inner + lax.axis_index("inner")
    x = lax.rem(me, 2)
    pair = me // 2
    z = LINE - 1 - lax.rem(pair, LINE)

    def dev(steps, to_x):
        s = lax.rem(pair + steps + pairs, pairs) * 2 + to_x
        return (s // inner, lax.rem(s, inner))

    partner = dev(0, 1 - x)
    up = dev(-1, x)
    down = dev(1, x)
    ahead = dev(-3, x)
    behind = dev(3, x)
    low = z >= 1
    high = z <= LINE - 2

    ins = (q_ref, g_ref, k_ref, v_ref)
    outs = (dq_ref, dk_ref, dv_ref)

    def cols(side, c):
        return pl.ds(pl.multiple_of((side * half + c) * HD, HD), HD)

    my_rows = pl.ds(pl.multiple_of(x * tok, tok), tok)
    other_rows = pl.ds(pl.multiple_of((1 - x) * tok, tok), tok)

    def landing(i, c):
        return qg.at[0, c, i, my_rows, :] if i < 2 else kv.at[c, i - 2, my_rows, :]

    def local_in(i, c):
        return pltpu.make_async_copy(ins[i].at[:, cols(x, c)], landing(i, c), xloc.at[c, i])

    def cross_in(i, c):
        return pltpu.make_async_remote_copy(
            ins[i].at[:, cols(1 - x, c)], landing(i, c), xsend.at[c, i], xrecv.at[c, i],
            device_id=partner, device_id_type=MESH)

    def local_out(i, c):
        return pltpu.make_async_copy(
            fin.at[c, i, my_rows, :], outs[i].at[:, cols(x, c)], oloc.at[c, i])

    def cross_out(i, c):
        return pltpu.make_async_remote_copy(
            fin.at[c, i, other_rows, :], outs[i].at[:, cols(x, c)], osend.at[c, i],
            orecv.at[c, i], device_id=partner, device_id_type=MESH)

    def forward(c, src, dst, sem, to, rows=None):
        rows = pl.ds(0, rows or size)
        return pltpu.make_async_remote_copy(
            qg.at[src, c, :, rows, :], qg.at[dst, c, :, rows, :], fsend.at[c, sem], frecv.at[c, dst - 1],
            device_id=to, device_id_type=MESH)

    def back(c, d, dst, to, rows=None):
        rows = pl.ds(0, rows or size)
        return pltpu.make_async_remote_copy(
            rout.at[d - 1, c, rows, :], slot.at[dst, c, rows, :], rsend.at[c, d - 1], rrecv.at[c, dst],
            device_id=to, device_id_type=MESH)

    def partial(c, d):
        return pltpu.make_async_remote_copy(
            part_out.at[c, d], part_in.at[c, d], psend.at[c, d - 1], precv.at[c, d - 1],
            device_id=dev(d, x), device_id_type=MESH)

    def totals(c, d):
        return pltpu.make_async_remote_copy(
            whole_out.at[c], whole_in.at[c, d], tsend.at[c, d - 1], trecv.at[c, d - 1],
            device_id=dev(-d, x), device_id_type=MESH)

    def arrived(c, d, rows=None):
        forward(c, 0, d, 0, up, rows).wait_recv()

    def returned(c, dst, rows=None):
        back(c, 1, dst, up, rows).wait_recv()

    def every_chunk(body):
        def step(c, carry):
            body(c)
            return carry
        lax.fori_loop(0, chunks, step, 0)

    @every_chunk
    def _(c):
        for i in range(4):
            local_in(i, c).start()

    barrier = pltpu.get_barrier_semaphore()
    for target in [partner] + [dev(d, x) for d in (-3, -2, -1, 1, 2, 3)]:
        pl.semaphore_signal(barrier, inc=1, device_id=target, device_id_type=MESH)
    pl.semaphore_wait(barrier, 7)

    @every_chunk
    def _(c):
        for i in range(4):
            cross_in(i, c).start()

    def when(*conds):
        return pl.when(functools.reduce(jnp.logical_and, conds))

    def stage_a(c):
        for i in range(2):
            local_in(i, c).wait()
            cross_in(i, c).wait_recv()

        @when(high)
        def _():
            forward(c, 0, 1, 0, up).start()

        @when(z >= 2)
        def _():
            forward(c, 0, 3, 1, ahead).start()

        @when(z == 1)
        def _():
            forward(c, 0, 3, 1, ahead, tok).start()

    def stage_b1(c):
        @when(low)
        def _():
            arrived(c, 1)

            @when(high)
            def _():
                forward(c, 1, 2, 2, up).start()

        @when(z == 0)
        def _():
            arrived(c, 3, tok)

        @when(low, high)
        def _():
            arrived(c, 3)
            forward(c, 3, 2, 3, down).start()

    def stage_b2(c):
        arrived(c, 2)

        @when(z == 2)
        def _():
            forward(c, 2, 3, 4, up, tok).start()

        @when(z == 1)
        def _():
            forward(c, 2, 1, 4, down).start()

    def stage_c(c):
        for i in range(2, 4):
            local_in(i, c).wait()
            cross_in(i, c).wait_recv()

        @when(z == LINE - 1)
        def _():
            arrived(c, 3, tok)

        @when(z == 0)
        def _():
            arrived(c, 1)

        width = window[0]
        key_all, value_all = kv[c, 0], kv[c, 1]
        for d in range(4):
            rows, top = (size, 0) if d < 3 else (tok, tok)
            logits = dot(key_all[top:], qg[d, c, 0, :rows, :], NT) * scale
            shape = (rows, rows)
            delta = (
                lax.broadcasted_iota(jnp.int32, shape, 1)
                - lax.broadcasted_iota(jnp.int32, shape, 0)
                + (d * size - top)
            )
            reach = jnp.where(pair + d < pairs, width, 0)
            allowed = (delta >= 0) & (delta < reach) if d == 0 else delta < reach
            weights = jnp.where(allowed, jnp.exp(logits), 0.0)
            prob_grad = dot(value_all[top:], qg[d, c, 1, :rows, :], NT)
            w_s[c, d, :rows, :rows] = weights
            p_s[c, d, :rows, :rows] = prob_grad
            norm = jnp.sum(weights, axis=0, keepdims=True)
            mixed = jnp.sum(weights * prob_grad, axis=0, keepdims=True)
            if d == 3:
                part_out[c, d] = jnp.zeros((2, size), jnp.float32)
            part_out[c, d, 0:1, :rows] = norm
            part_out[c, d, 1:2, :rows] = mixed
            if d > 0:
                partial(c, d).start()

    def stage_s1(c):
        for d in range(1, 4):
            partial(c, d).wait_recv()
        sums = part_out[c, 0] + part_in[c, 1] + part_in[c, 2] + part_in[c, 3]
        inverse = 1.0 / sums[0:1]
        whole_out[c, 0:1] = inverse
        whole_out[c, 1:2] = sums[1:2] * inverse
        for d in range(1, 4):
            totals(c, d).start()

    def stage_s2(c):
        for d in range(1, 4):
            totals(c, d).wait_recv()
        key_all = kv[c, 0]
        key_total = jnp.zeros((size, HD), jnp.float32)
        value_total = jnp.zeros((size, HD), jnp.float32)
        for d in (3, 2, 1, 0):
            rows, top = (size, 0) if d < 3 else (tok, tok)
            stats = whole_in[c, d] if d else whole_out[c]
            probs = w_s[c, d, :rows, :rows] * stats[0:1, :rows]
            logit_grad = probs * (p_s[c, d, :rows, :rows] - stats[1:2, :rows])
            logit_grad = logit_grad.astype(jnp.bfloat16)
            value_part = dot(probs.astype(jnp.bfloat16), qg[d, c, 1, :rows, :], NN)
            key_part = dot(logit_grad, qg[d, c, 0, :rows, :], NN)
            if d == 3:
                acc[c, d, rows:, :] = jnp.zeros((size - rows, HD), jnp.float32)
                rest = jnp.zeros((top, HD), jnp.float32)
                value_part = jnp.concatenate([rest, value_part], axis=0)
                key_part = jnp.concatenate([rest, key_part], axis=0)
            value_total = value_total + value_part
            key_total = key_total + key_part
            acc[c, d, :rows, :] = dot(logit_grad, key_all[top:], TN) * scale
        fin[c, 1] = (key_total * scale).astype(jnp.bfloat16)
        fin[c, 2] = value_total.astype(jnp.bfloat16)

        @when(z == LINE - 1)
        def _():
            rout[2, c] = acc[c, 3].astype(jnp.bfloat16)
            back(c, 3, 2, down, tok).start()

        @when(z == 0)
        def _():
            rout[0, c] = acc[c, 1].astype(jnp.bfloat16)
            back(c, 1, 2, up).start()

        for i in range(1, 3):
            local_out(i, c).start()
            cross_out(i, c).start()

    def fold(c, d, source, rows=None):
        rows = rows or size
        returned(c, source, rows)
        rout[d - 1, c, :rows] = (
            acc[c, d, :rows] + slot[source, c, :rows].astype(jnp.float32)
        ).astype(jnp.bfloat16)
        if rows < size:
            rout[d - 1, c, rows:] = acc[c, d, rows:].astype(jnp.bfloat16)

    def plain(c, d):
        rout[d - 1, c] = acc[c, d].astype(jnp.bfloat16)

    def stage_r2(c):
        @when(z == 0)
        def _():
            plain(c, 2)
            back(c, 2, 3, up).start()

        @when(z == 1)
        def _():
            fold(c, 2, 2)
            back(c, 2, 3, up).start()

        @when(z == 2)
        def _():
            fold(c, 2, 2, tok)
            back(c, 2, 1, down).start()

        @when(z == 3)
        def _():
            plain(c, 2)
            back(c, 2, 1, down).start()

    def stage_r1(c):
        @when(z == LINE - 1)
        def _():
            plain(c, 1)
            back(c, 1, 0, down).start()

        @when(low, high)
        def _():
            fold(c, 1, 1)
            back(c, 1, 0, down).start()
            fold(c, 3, 3)
            back(c, 3, 4, behind).start()

        @when(z == 0)
        def _():
            plain(c, 3)
            back(c, 3, 4, behind, tok).start()

    def stage_r0(c):
        @when(high)
        def _():
            returned(c, 0)
            acc[c, 0] = acc[c, 0] + slot[0, c].astype(jnp.float32)

        @when(z >= 2)
        def _():
            returned(c, 4)
            acc[c, 0] = acc[c, 0] + slot[4, c].astype(jnp.float32)

        @when(z == 1)
        def _():
            returned(c, 4, tok)
            acc[c, 0, :tok] = acc[c, 0, :tok] + slot[4, c, :tok].astype(jnp.float32)

        fin[c, 0] = acc[c, 0].astype(jnp.bfloat16)
        local_out(0, c).start()
        cross_out(0, c).start()

    stages = (
        stage_a, stage_b1, stage_b2, stage_c, stage_s1, stage_s2, stage_r2, stage_r1, stage_r0
    )

    def tick(t, carry):
        for lag, stage in enumerate(stages):
            c = t - lag

            @when(c >= 0, c < chunks)
            def _():
                stage(c)
        return carry

    lax.fori_loop(0, chunks + len(stages) - 1, tick, 0)

    @every_chunk
    def _(c):
        for i in range(4):
            cross_in(i, c).wait_send()
        for i in range(3):
            local_out(i, c).wait()
            cross_out(i, c).wait()

        @when(high)
        def _():
            forward(c, 0, 1, 0, up).wait_send()

        @when(z >= 2)
        def _():
            forward(c, 0, 3, 1, ahead).wait_send()

        @when(z == 1)
        def _():
            forward(c, 0, 3, 1, ahead, tok).wait_send()
            forward(c, 2, 1, 4, down).wait_send()

        @when(z == 2)
        def _():
            forward(c, 2, 3, 4, up, tok).wait_send()

        @when(low, high)
        def _():
            forward(c, 1, 2, 2, up).wait_send()
            forward(c, 3, 2, 3, down).wait_send()
            back(c, 3, 0, up).wait_send()

        @when(jnp.logical_not(jnp.logical_and(low, high)))
        def _():
            back(c, 3, 0, up, tok).wait_send()
        for d in range(1, 4):
            if d < 3:
                back(c, d, 0, up).wait_send()
            partial(c, d).wait_send()
            totals(c, d).wait_send()


def per_device(queries, keys, values, grad_out, window):
    outer, inner = lax.axis_size("outer"), lax.axis_size("inner")
    tok, columns = queries.shape
    heads = columns // HD
    chunks = heads // 2
    size = 2 * tok
    low, full = jnp.bfloat16, jnp.float32
    vmem = pl.BlockSpec(memory_space=pltpu.VMEM)
    block = (chunks, 2, size, HD)
    sums = (chunks, size, HD)
    sems = (4, 4, 4, 5, 3, 3, 5, 3, 3, 3, 3, 3, 3, 3)
    return pl.pallas_call(
        functools.partial(kernel, (outer, inner, tok, heads)),
        out_shape=[jax.ShapeDtypeStruct((tok, columns), low)] * 3,
        in_specs=[pl.BlockSpec(memory_space=pltpu.SMEM)] + [vmem] * 4,
        out_specs=[vmem] * 3,
        scratch_shapes=[
            pltpu.VMEM((4,) + block, low),
            pltpu.VMEM(block, low),
            pltpu.VMEM((5,) + sums, low),
            pltpu.VMEM((3,) + sums, low),
            pltpu.VMEM((chunks, 4, size, HD), full),
            pltpu.VMEM((chunks, 3, size, HD), low),
            pltpu.VMEM((chunks, 4, size, size), full),
            pltpu.VMEM((chunks, 4, size, size), full),
            pltpu.VMEM((chunks, 4, 2, size), full),
            pltpu.VMEM((chunks, 4, 2, size), full),
            pltpu.VMEM((chunks, 2, size), full),
            pltpu.VMEM((chunks, 4, 2, size), full),
        ] + [pltpu.SemaphoreType.DMA((chunks, n)) for n in sems],
        compiler_params=pltpu.CompilerParams(
            collective_id=0, has_side_effects=True, vmem_limit_bytes=56 * 2**20
        ),
    )(window, queries, keys, values, grad_out)


def solution(mesh):
    rows = P(("outer", "inner"), None)
    return jax.shard_map(
        per_device,
        mesh=mesh,
        in_specs=(rows, rows, rows, rows, P()),
        out_specs=(rows, rows, rows),
        check_vma=False,
    )
```

```python
import functools

import jax
import jax.numpy as jnp
from jax import lax
from jax.experimental import pallas as pl
from jax.experimental.pallas import tpu as pltpu
from jax.sharding import PartitionSpec as P

HD = 128
LINE = 4
MESH = pl.DeviceIdType.MESH
NT = (((1,), (1,)), ((), ()))
NN = (((1,), (0,)), ((), ()))
TN = (((0,), (0,)), ((), ()))


def dot(a, b, dims):
    return lax.dot_general(a, b, dims, preferred_element_type=jnp.float32)


def kernel(
    sizes, window, q_ref, k_ref, v_ref, g_ref, dq_ref, dk_ref, dv_ref,
    qg, kv, slot, rout, acc, fin, w_s, p_s, part_out, part_in, whole_out, whole_in,
    xsend, xrecv, xloc, fsend, frecv, rsend, rrecv, osend, orecv, oloc, psend, precv, tsend, trecv,
):
    outer, inner, tok, heads = sizes
    half = heads // 2
    chunks = half
    size = 2 * tok
    scale = HD ** -0.5
    total = outer * inner
    pairs = total // 2
    me = lax.axis_index("outer") * inner + lax.axis_index("inner")
    x = lax.rem(me, 2)
    pair = me // 2
    z = LINE - 1 - lax.rem(pair, LINE)

    def dev(steps, to_x):
        s = lax.rem(pair + steps + pairs, pairs) * 2 + to_x
        return (s // inner, lax.rem(s, inner))

    partner = dev(0, 1 - x)
    up = dev(-1, x)
    down = dev(1, x)
    ahead = dev(-3, x)
    behind = dev(3, x)
    low = z >= 1
    high = z <= LINE - 2

    ins = (q_ref, g_ref, k_ref, v_ref)
    outs = (dq_ref, dk_ref, dv_ref)

    def cols(side, c):
        return pl.ds(pl.multiple_of((side * half + c) * HD, HD), HD)

    my_rows = pl.ds(pl.multiple_of(x * tok, tok), tok)
    other_rows = pl.ds(pl.multiple_of((1 - x) * tok, tok), tok)

    def landing(i, c):
        return qg.at[0, c, i, my_rows, :] if i < 2 else kv.at[c, i - 2, my_rows, :]

    def local_in(i, c):
        return pltpu.make_async_copy(ins[i].at[:, cols(x, c)], landing(i, c), xloc.at[c, i])

    def cross_in(i, c):
        return pltpu.make_async_remote_copy(
            ins[i].at[:, cols(1 - x, c)], landing(i, c), xsend.at[c, i], xrecv.at[c, i],
            device_id=partner, device_id_type=MESH)

    def local_out(i, c):
        return pltpu.make_async_copy(
            fin.at[c, i, my_rows, :], outs[i].at[:, cols(x, c)], oloc.at[c, i])

    def cross_out(i, c):
        return pltpu.make_async_remote_copy(
            fin.at[c, i, other_rows, :], outs[i].at[:, cols(x, c)], osend.at[c, i],
            orecv.at[c, i], device_id=partner, device_id_type=MESH)

    def forward(c, src, dst, sem, to, rows=None):
        rows = pl.ds(0, rows or size)
        return pltpu.make_async_remote_copy(
            qg.at[src, c, :, rows, :], qg.at[dst, c, :, rows, :], fsend.at[c, sem], frecv.at[c, dst - 1],
            device_id=to, device_id_type=MESH)

    def back(c, d, dst, to, rows=None):
        rows = pl.ds(0, rows or size)
        return pltpu.make_async_remote_copy(
            rout.at[d - 1, c, rows, :], slot.at[dst, c, rows, :], rsend.at[c, d - 1], rrecv.at[c, dst],
            device_id=to, device_id_type=MESH)

    def partial(c, d):
        return pltpu.make_async_remote_copy(
            part_out.at[c, d], part_in.at[c, d], psend.at[c, d - 1], precv.at[c, d - 1],
            device_id=dev(d, x), device_id_type=MESH)

    def totals(c, d):
        return pltpu.make_async_remote_copy(
            whole_out.at[c], whole_in.at[c, d], tsend.at[c, d - 1], trecv.at[c, d - 1],
            device_id=dev(-d, x), device_id_type=MESH)

    def arrived(c, d, rows=None):
        forward(c, 0, d, 0, up, rows).wait_recv()

    def returned(c, dst, rows=None):
        back(c, 1, dst, up, rows).wait_recv()

    def every_chunk(body):
        def step(c, carry):
            body(c)
            return carry
        lax.fori_loop(0, chunks, step, 0)

    @every_chunk
    def _(c):
        for i in range(4):
            local_in(i, c).start()

    barrier = pltpu.get_barrier_semaphore()
    for target in [partner] + [dev(d, x) for d in (-3, -2, -1, 1, 2, 3)]:
        pl.semaphore_signal(barrier, inc=1, device_id=target, device_id_type=MESH)
    pl.semaphore_wait(barrier, 7)

    @every_chunk
    def _(c):
        for i in range(4):
            cross_in(i, c).start()

    def when(*conds):
        return pl.when(functools.reduce(jnp.logical_and, conds))

    def stage_a(c):
        for i in range(2):
            local_in(i, c).wait()
            cross_in(i, c).wait_recv()

        @when(high)
        def _():
            forward(c, 0, 1, 0, up).start()

        @when(z >= 2)
        def _():
            forward(c, 0, 3, 1, ahead).start()

        @when(z == 1)
        def _():
            forward(c, 0, 3, 1, ahead, tok).start()

    def stage_b1(c):
        @when(low)
        def _():
            arrived(c, 1)

            @when(high)
            def _():
                forward(c, 1, 2, 2, up).start()

        @when(z == 0)
        def _():
            arrived(c, 3, tok)

        @when(low, high)
        def _():
            arrived(c, 3)
            forward(c, 3, 2, 3, down).start()

    def stage_b2(c):
        arrived(c, 2)

        @when(z == 2)
        def _():
            forward(c, 2, 3, 4, up, tok).start()

        @when(z == 1)
        def _():
            forward(c, 2, 1, 4, down).start()

    def stage_c(c):
        for i in range(2, 4):
            local_in(i, c).wait()
            cross_in(i, c).wait_recv()

        @when(z == LINE - 1)
        def _():
            arrived(c, 3, tok)

        @when(z == 0)
        def _():
            arrived(c, 1)

        width = window[0]
        key_all, value_all = kv[c, 0], kv[c, 1]
        for d in range(4):
            rows, top = (size, 0) if d < 3 else (tok, tok)
            logits = dot(key_all[top:], qg[d, c, 0, :rows, :], NT) * scale
            shape = (rows, rows)
            delta = (
                lax.broadcasted_iota(jnp.int32, shape, 1)
                - lax.broadcasted_iota(jnp.int32, shape, 0)
                + (d * size - top)
            )
            reach = jnp.where(pair + d < pairs, width, 0)
            allowed = (delta >= 0) & (delta < reach) if d == 0 else delta < reach
            weights = jnp.where(allowed, jnp.exp(logits), 0.0)
            prob_grad = dot(value_all[top:], qg[d, c, 1, :rows, :], NT)
            w_s[c, d, :rows, :rows] = weights
            p_s[c, d, :rows, :rows] = prob_grad
            norm = jnp.sum(weights, axis=0, keepdims=True)
            mixed = jnp.sum(weights * prob_grad, axis=0, keepdims=True)
            if d == 3:
                part_out[c, d] = jnp.zeros((2, size), jnp.float32)
            part_out[c, d, 0:1, :rows] = norm
            part_out[c, d, 1:2, :rows] = mixed
            if d > 0:
                partial(c, d).start()

    def stage_s1(c):
        for d in range(1, 4):
            partial(c, d).wait_recv()
        sums = part_out[c, 0] + part_in[c, 1] + part_in[c, 2] + part_in[c, 3]
        inverse = 1.0 / sums[0:1]
        whole_out[c, 0:1] = inverse
        whole_out[c, 1:2] = sums[1:2] * inverse
        for d in range(1, 4):
            totals(c, d).start()

    def stage_s2(c):
        for d in range(1, 4):
            totals(c, d).wait_recv()
        key_all = kv[c, 0]
        key_total = jnp.zeros((size, HD), jnp.float32)
        value_total = jnp.zeros((size, HD), jnp.float32)
        for d in (3, 2, 1, 0):
            rows, top = (size, 0) if d < 3 else (tok, tok)
            stats = whole_in[c, d] if d else whole_out[c]
            probs = w_s[c, d, :rows, :rows] * stats[0:1, :rows]
            logit_grad = probs * (p_s[c, d, :rows, :rows] - stats[1:2, :rows])
            logit_grad = logit_grad.astype(jnp.bfloat16)
            value_part = dot(probs.astype(jnp.bfloat16), qg[d, c, 1, :rows, :], NN)
            key_part = dot(logit_grad, qg[d, c, 0, :rows, :], NN)
            if d == 3:
                acc[c, d, rows:, :] = jnp.zeros((size - rows, HD), jnp.float32)
                rest = jnp.zeros((top, HD), jnp.float32)
                value_part = jnp.concatenate([rest, value_part], axis=0)
                key_part = jnp.concatenate([rest, key_part], axis=0)
            value_total = value_total + value_part
            key_total = key_total + key_part
            acc[c, d, :rows, :] = dot(logit_grad, key_all[top:], TN) * scale
        fin[c, 1] = (key_total * scale).astype(jnp.bfloat16)
        fin[c, 2] = value_total.astype(jnp.bfloat16)

        @when(z == LINE - 1)
        def _():
            rout[2, c] = acc[c, 3].astype(jnp.bfloat16)
            back(c, 3, 2, down, tok).start()

        @when(z == 0)
        def _():
            rout[0, c] = acc[c, 1].astype(jnp.bfloat16)
            back(c, 1, 2, up).start()

        for i in range(1, 3):
            local_out(i, c).start()
            cross_out(i, c).start()

    def fold(c, d, source, rows=None):
        rows = rows or size
        returned(c, source, rows)
        rout[d - 1, c, :rows] = (
            acc[c, d, :rows] + slot[source, c, :rows].astype(jnp.float32)
        ).astype(jnp.bfloat16)
        if rows < size:
            rout[d - 1, c, rows:] = acc[c, d, rows:].astype(jnp.bfloat16)

    def plain(c, d):
        rout[d - 1, c] = acc[c, d].astype(jnp.bfloat16)

    def stage_r2(c):
        @when(z == 0)
        def _():
            plain(c, 2)
            back(c, 2, 3, up).start()

        @when(z == 1)
        def _():
            fold(c, 2, 2)
            back(c, 2, 3, up).start()

        @when(z == 2)
        def _():
            fold(c, 2, 2, tok)
            back(c, 2, 1, down).start()

        @when(z == 3)
        def _():
            plain(c, 2)
            back(c, 2, 1, down).start()

    def stage_r1(c):
        @when(z == LINE - 1)
        def _():
            plain(c, 1)
            back(c, 1, 0, down).start()

        @when(low, high)
        def _():
            fold(c, 1, 1)
            back(c, 1, 0, down).start()
            fold(c, 3, 3)
            back(c, 3, 4, behind).start()

        @when(z == 0)
        def _():
            plain(c, 3)
            back(c, 3, 4, behind, tok).start()

    def stage_r0(c):
        @when(high)
        def _():
            returned(c, 0)
            acc[c, 0] = acc[c, 0] + slot[0, c].astype(jnp.float32)

        @when(z >= 2)
        def _():
            returned(c, 4)
            acc[c, 0] = acc[c, 0] + slot[4, c].astype(jnp.float32)

        @when(z == 1)
        def _():
            returned(c, 4, tok)
            acc[c, 0, :tok] = acc[c, 0, :tok] + slot[4, c, :tok].astype(jnp.float32)

        fin[c, 0] = acc[c, 0].astype(jnp.bfloat16)
        local_out(0, c).start()
        cross_out(0, c).start()

    schedule = (
        (stage_a, 0),
        (stage_b1, 1),
        (stage_b2, 2),
        (stage_c, 3),
        (stage_s1, 4),
        (stage_s2, 5),
        (stage_r2, 6),
        (stage_r1, 7),
        (stage_r0, 8),
    )

    def tick(t, carry):
        for stage, lag in schedule:
            c = t - lag

            @when(c >= 0, c < chunks)
            def _():
                stage(c)
        return carry

    lax.fori_loop(0, chunks + max(lag for _, lag in schedule), tick, 0)

    @every_chunk
    def _(c):
        for i in range(4):
            cross_in(i, c).wait_send()
        for i in range(3):
            local_out(i, c).wait()
            cross_out(i, c).wait()

        @when(high)
        def _():
            forward(c, 0, 1, 0, up).wait_send()

        @when(z >= 2)
        def _():
            forward(c, 0, 3, 1, ahead).wait_send()

        @when(z == 1)
        def _():
            forward(c, 0, 3, 1, ahead, tok).wait_send()
            forward(c, 2, 1, 4, down).wait_send()

        @when(z == 2)
        def _():
            forward(c, 2, 3, 4, up, tok).wait_send()

        @when(low, high)
        def _():
            forward(c, 1, 2, 2, up).wait_send()
            forward(c, 3, 2, 3, down).wait_send()
            back(c, 3, 0, up).wait_send()

        @when(jnp.logical_not(jnp.logical_and(low, high)))
        def _():
            back(c, 3, 0, up, tok).wait_send()
        for d in range(1, 4):
            if d < 3:
                back(c, d, 0, up).wait_send()
            partial(c, d).wait_send()
            totals(c, d).wait_send()


def per_device(queries, keys, values, grad_out, window):
    outer, inner = lax.axis_size("outer"), lax.axis_size("inner")
    tok, columns = queries.shape
    heads = columns // HD
    chunks = heads // 2
    size = 2 * tok
    low, full = jnp.bfloat16, jnp.float32
    block = (chunks, 2, size, HD)
    sums = (chunks, size, HD)
    sems = (4, 4, 4, 5, 3, 3, 5, 3, 3, 3, 3, 3, 3, 3)
    return pl.pallas_call(
        functools.partial(kernel, (outer, inner, tok, heads)),
        out_shape=[jax.ShapeDtypeStruct((tok, columns), low)] * 3,
        in_specs=[pl.BlockSpec(memory_space=pltpu.SMEM)] + [pl.BlockSpec(memory_space=pl.ANY)] * 4,
        out_specs=[pl.BlockSpec(memory_space=pl.ANY)] * 3,
        scratch_shapes=[
            pltpu.VMEM((4,) + block, low),
            pltpu.VMEM(block, low),
            pltpu.VMEM((5,) + sums, low),
            pltpu.VMEM((3,) + sums, low),
            pltpu.VMEM((chunks, 4, size, HD), full),
            pltpu.VMEM((chunks, 3, size, HD), low),
            pltpu.VMEM((chunks, 4, size, size), full),
            pltpu.VMEM((chunks, 4, size, size), full),
            pltpu.VMEM((chunks, 4, 2, size), full),
            pltpu.VMEM((chunks, 4, 2, size), full),
            pltpu.VMEM((chunks, 2, size), full),
            pltpu.VMEM((chunks, 4, 2, size), full),
        ] + [pltpu.SemaphoreType.DMA((chunks, n)) for n in sems],
        compiler_params=pltpu.CompilerParams(
            collective_id=0, has_side_effects=True, vmem_limit_bytes=56 * 2**20
        ),
    )(window, queries, keys, values, grad_out)


def solution(mesh):
    rows = P(("outer", "inner"), None)
    return jax.shard_map(
        per_device,
        mesh=mesh,
        in_specs=(rows, rows, rows, rows, P()),
        out_specs=(rows, rows, rows),
        check_vma=False,
    )
```
